32 devices in a mesh: shots: 2 (over x), gx: 16 (over z, y, core).
Axes of the slice: x: 2, y: 2, z: 4, core: 2. Of those that a mesh axis runs over, the one named last changes fastest.
Arguments:
- velocity: float32 [256, 24, 128], P('gx'), may hold values from 0.05 to 0.18
- source_prior: float32 [512, 24, 128], P(('shots', 'gx')), parts along dimension 0, may hold values from -6 to 6
- source_now: float32 [512, 24, 128], P(('shots', 'gx')), parts along dimension 0, may hold values from -6 to 6
- record_prior: float32 [512, 24, 128], P(('shots', 'gx')), parts along dimension 0, may hold values from -6 to 6
- record_now: float32 [512, 24, 128], P(('shots', 'gx')), parts along dimension 0, may hold values from -6 to 6
- source_inline: int32 [32], P('shots'), parts along dimension 0, may hold values from 0 to 255
- source_crossline: int32 [32], P('shots'), parts along dimension 0, may hold values from 0 to 23
- source_pulse: float32 [32, 2], P('shots'), parts along dimension 0, may hold values from -12 to 12
- receiver_inline: int32 [2048], P('shots'), parts along dimension 0, may hold values from 0 to 255
- receiver_crossline: int32 [2048], P('shots'), parts along dimension 0, may hold values from 0 to 23
- receiver_trace: float32 [2048, 2], P('shots'), parts along dimension 0, may hold values from -12 to 12
- offsets: int32 [17], replicated, may hold values from -8 to 8
Outputs:
- images: bfloat16 [34, 256, 24, 128], P('shots', 'gx'), parts along dimension 0
- adjoint_source: float32 [512, 24, 128], P(('shots', 'gx')), parts along dimension 0
- adjoint_receiver: float32 [512, 24, 128], P(('shots', 'gx')), parts along dimension 0
The draws below stay inside these ranges and needn't reach their ends.
There are 2 independent parts, one for each index of `shots`. The reference program is written for one: setup_inputs(seed, part) draws one part's arguments, and reference() takes and returns one part's arrays. A program takes and returns all parts, laid end to end along the dimension named above; an argument that names none is the same for every part. Nothing has to cross between parts.
All inputs are finite; a program needn't handle non-finite values.
Results may differ from the reference program's by a relative error of at most 0.001.
Values sent between devices are 32-bit elements; how exact they have to be, the bound alone decides.
No kernel may reach another device: no remote copies, remote signals or barrier semaphores. Data moves between devices by JAX's collectives and lax.ppermute only.
A program may use at most 128 MiB of HBM per device.

```python
import jax
import jax.numpy as jnp
from jax import lax

NY = 24
NZ = 128
STEPS = 2
NLAG = 17
LAG_MAX = 8
NSRC = 16
NREC = 1024
NX = 256


def with_ends(drawn, key, smallest, top_value):
    longest = drawn.shape.index(max(drawn.shape))
    spots = []
    for shift in (0, 1):
        where = [jax.random.randint(jax.random.fold_in(key, axis), (), 0, length) for axis, length in enumerate(drawn.shape)]
        where[longest] = (where[longest] + shift) % drawn.shape[longest]
        spots.append(tuple(where))
    return drawn.at[spots[0]].set(smallest).at[spots[1]].set(top_value)


def block_levels(rng, dims, split, smallest, top_value):
    def one(axis_at, blocks):
        draws = jax.random.uniform(jax.random.fold_in(jax.random.fold_in(rng, 6), axis_at), (blocks,), jnp.float32, smallest / len(split), top_value / len(split))
        return jnp.repeat(jnp.exp(draws), dims[axis_at] // blocks).reshape((-1,) + (1,) * (len(dims) - axis_at - 1))

    level = one(*split[0])
    for cut in split[1:]:
        level = level * one(*cut)
    return level


def centred(rng, shape, width, limit, pieces=(), held_as=jnp.bfloat16):
    result = width * jax.random.normal(rng, shape, jnp.float32)
    if pieces:
        result = result * block_levels(rng, shape, pieces, -0.22, 0.18)
    return jnp.clip(result, -limit, limit).astype(held_as)


def setup_inputs(seed: int = 0, part: int = 0) -> dict:
    keys = jax.random.split(jax.random.key(seed), 13)
    own_keys = jax.random.split(jax.random.fold_in(keys[12], part), 13)
    velocity = jnp.clip(0.05 + 0.13000001 * jax.random.uniform(keys[0], (NX, NY, NZ), jnp.float32) ** block_levels(keys[0], (NX, NY, NZ), ((0, 16),), -0.2, 0.2), 0.05, 0.18)
    source_prior = centred(own_keys[1], (NX, NY, NZ), 1.0, 6.0, ((0, 16),), jnp.float32)
    source_now = centred(own_keys[2], (NX, NY, NZ), 1.0, 6.0, ((0, 16),), jnp.float32)
    record_prior = centred(own_keys[3], (NX, NY, NZ), 1.0, 6.0, ((0, 16),), jnp.float32)
    record_now = centred(own_keys[4], (NX, NY, NZ), 1.0, 6.0, ((0, 16),), jnp.float32)
    source_inline = with_ends(jax.random.randint(own_keys[5], (NSRC,), 0, NX), jax.random.fold_in(own_keys[5], 1), 0, NX - 1).astype(jnp.int32)
    source_crossline = with_ends(jax.random.randint(own_keys[6], (NSRC,), 0, NY), jax.random.fold_in(own_keys[6], 1), 0, NY - 1).astype(jnp.int32)
    source_pulse = centred(own_keys[7], (NSRC, STEPS), 2.0, 12.0, (), jnp.float32)
    receiver_inline = with_ends(jax.random.randint(own_keys[8], (NREC,), 0, NX), jax.random.fold_in(own_keys[8], 1), 0, NX - 1).astype(jnp.int32)
    receiver_crossline = with_ends(jax.random.randint(own_keys[9], (NREC,), 0, NY), jax.random.fold_in(own_keys[9], 1), 0, NY - 1).astype(jnp.int32)
    receiver_trace = centred(own_keys[10], (NREC, STEPS), 2.0, 12.0, (), jnp.float32)
    offsets = with_ends(jax.random.randint(keys[11], (NLAG,), -LAG_MAX, LAG_MAX + 1), jax.random.fold_in(keys[11], 1), -LAG_MAX, LAG_MAX).astype(jnp.int32)
    return {"velocity": velocity, "source_prior": source_prior, "source_now": source_now, "record_prior": record_prior, "record_now": record_now, "source_inline": source_inline, "source_crossline": source_crossline, "source_pulse": source_pulse, "receiver_inline": receiver_inline, "receiver_crossline": receiver_crossline, "receiver_trace": receiver_trace, "offsets": offsets}


stencil = (-205.0 / 72.0, 8.0 / 5.0, -1.0 / 5.0, 8.0 / 315.0, -1.0 / 560.0)
source_depth = 3
record_depth = 1


def laplace(field):
    cells_x, cells_y, cells_z = field.shape
    padded = jnp.pad(field, 4)
    summed = 3.0 * stencil[0] * field
    for offset in range(1, 5):
        beside_all = padded[4 + offset:4 + offset + cells_x, 4:4 + cells_y, 4:4 + cells_z]
        beside_all = beside_all + padded[4 - offset:4 - offset + cells_x, 4:4 + cells_y, 4:4 + cells_z]
        beside_all = beside_all + padded[4:4 + cells_x, 4 + offset:4 + offset + cells_y, 4:4 + cells_z]
        beside_all = beside_all + padded[4:4 + cells_x, 4 - offset:4 - offset + cells_y, 4:4 + cells_z]
        beside_all = beside_all + padded[4:4 + cells_x, 4:4 + cells_y, 4 + offset:4 + offset + cells_z]
        beside_all = beside_all + padded[4:4 + cells_x, 4:4 + cells_y, 4 - offset:4 - offset + cells_z]
        summed = summed + stencil[offset] * beside_all
    return summed


def injection(place_x, place_y, amplitude, count_x, count_y):
    hits_x = (place_x[:, None] == jnp.arange(count_x, dtype=jnp.int32)[None, :]).astype(jnp.float32) * amplitude[:, None]
    hits_y = (place_y[:, None] == jnp.arange(count_y, dtype=jnp.int32)[None, :]).astype(jnp.float32)
    return jnp.einsum("sx,sy->xy", hits_x, hits_y, precision=lax.Precision.HIGHEST)


def reference(velocity, source_prior, source_now, record_prior, record_now, source_inline, source_crossline, source_pulse, receiver_inline, receiver_crossline, receiver_trace, offsets):
    cells_x, cells_y, cells_z = velocity.shape
    for moment in range(STEPS):
        source_next = 2.0 * source_now - source_prior + velocity * laplace(source_now)
        source_next = source_next.at[:, :, source_depth].add(injection(source_inline, source_crossline, source_pulse[:, moment], cells_x, cells_y))
        record_next = 2.0 * record_now - record_prior + velocity * laplace(record_now)
        record_next = record_next.at[:, :, record_depth].add(injection(receiver_inline, receiver_crossline, receiver_trace[:, moment], cells_x, cells_y))
        source_prior, source_now = source_now, source_next
        record_prior, record_now = record_now, record_next
    wide_source = jnp.pad(source_now, ((LAG_MAX, LAG_MAX), (0, 0), (0, 0)))
    wide_record = jnp.pad(record_now, ((LAG_MAX, LAG_MAX), (0, 0), (0, 0)))

    def single(shift_cells):
        left = lax.dynamic_slice_in_dim(wide_source, (LAG_MAX - shift_cells).astype(jnp.int32), cells_x, 0)
        right = lax.dynamic_slice_in_dim(wide_record, (LAG_MAX + shift_cells).astype(jnp.int32), cells_x, 0)
        return (left * right).astype(jnp.bfloat16)

    images = lax.map(single, offsets)
    squares_source = jnp.pad(source_now * source_now, ((2 * LAG_MAX, 2 * LAG_MAX), (0, 0), (0, 0)))
    squares_record = jnp.pad(record_now * record_now, ((2 * LAG_MAX, 2 * LAG_MAX), (0, 0), (0, 0)))
    weights = (offsets * offsets).astype(jnp.float32) / (LAG_MAX * LAG_MAX * NLAG)

    def accumulate(index, carry):
        toward_source, toward_record = carry
        shift_cells = offsets[index]
        weight = weights[index]
        from_record = lax.dynamic_slice_in_dim(squares_record, (2 * LAG_MAX + 2 * shift_cells).astype(jnp.int32), cells_x, 0)
        from_source = lax.dynamic_slice_in_dim(squares_source, (2 * LAG_MAX - 2 * shift_cells).astype(jnp.int32), cells_x, 0)
        return (toward_source + weight * from_record, toward_record + weight * from_source)

    empty = jnp.zeros(source_now.shape, jnp.float32)
    toward_source, toward_record = lax.fori_loop(0, NLAG, accumulate, (empty, empty))
    return images, source_now * toward_source, record_now * toward_record
```

```python
import functools

import jax
import jax.numpy as jnp
from jax import lax
from jax.experimental import pallas as pl
from jax.experimental.pallas import tpu as pltpu
from jax.sharding import PartitionSpec as P

STEPS = 2
LAG_MAX = 8
REACH = 4
PAD = 8

stencil = (-205.0 / 72.0, 8.0 / 5.0, -1.0 / 5.0, 8.0 / 315.0, -1.0 / 560.0)
source_depth = 3
record_depth = 1

VMEM = pl.BlockSpec(memory_space=pltpu.VMEM)
SMEM = pl.BlockSpec(memory_space=pltpu.SMEM)
ANY = pl.BlockSpec(memory_space=pl.ANY)


def params(mib):
    return pltpu.CompilerParams(vmem_limit_bytes=mib << 20)


def pack_kernel(ve, sp, sn, rp, rn, near, far, sems):
    extent = ve.shape[0]
    odd = lax.rem(lax.axis_index("gx"), 2)
    copies = []
    for out, right in ((near, 1 - odd), (far, odd)):
        at = 0
        for field, width in ((sn, 2 * REACH), (rn, 2 * REACH), (sp, REACH), (rp, REACH), (ve, REACH)):
            first = right * (extent - width)
            copies.append(
                pltpu.make_async_copy(
                    field.at[pl.ds(first, width)],
                    out.at[pl.ds(at, width)],
                    sems.at[len(copies)],
                )
            )
            at += width
    for c in copies:
        c.start()
    for c in copies:
        c.wait()


def shifted(u, k, lane):
    cells_z = u.shape[-1]
    rolled = pltpu.roll(u, k % cells_z, u.ndim - 1)
    inside = lane >= k if k > 0 else lane < cells_z + k
    return jnp.where(inside, rolled, 0.0)


def laplace_plane(u_ref, f, x, cells_y, lane):
    mid = u_ref[f, x, PAD : PAD + cells_y, :]
    total = 3.0 * stencil[0] * mid
    for k in range(1, 5):
        beside = u_ref[f, x + k, PAD : PAD + cells_y, :] + u_ref[f, x - k, PAD : PAD + cells_y, :]
        beside = beside + u_ref[f, x, PAD + k : PAD + k + cells_y, :]
        beside = beside + u_ref[f, x, PAD - k : PAD - k + cells_y, :]
        beside = beside + shifted(mid, k, lane)
        beside = beside + shifted(mid, -k, lane)
        total = total + stencil[k] * beside
    return mid, total


def source_plane(place_x, place_y, amplitude, first, cells_y):
    count = place_x.shape[1]
    row = lax.broadcasted_iota(jnp.int32, (128, count), 0)
    hit = (place_x - first) == lax.rem(row, 64)
    amp = jnp.where(row < 64, amplitude[0:1, :], amplitude[1:2, :])
    amp = jnp.where(hit, amp, 0.0)
    hit_y = (place_y == lax.broadcasted_iota(jnp.int32, (cells_y, count), 0)).astype(jnp.float32)
    return lax.dot_general(
        hit_y,
        amp,
        (((1,), (1,)), ((), ())),
        precision=lax.Precision.HIGHEST,
        preferred_element_type=jnp.float32,
    )


def step_kernel(
    ve, sp, sn, rp, rn, near, far, s_x, s_y, s_a, r_x, r_y, r_a, out, now, nxt, pri, vel, inj
):
    extent, cells_y, cells_z = ve.shape
    index = lax.axis_index("gx")
    odd = lax.rem(index, 2)
    first = index * extent - REACH
    lane = lax.broadcasted_iota(jnp.int32, (cells_y, cells_z), 1)
    inj[0] = source_plane(s_x[...], s_y[...], s_a[...], first, cells_y)
    inj[1] = source_plane(r_x[...], r_y[...], r_a[...], first, cells_y)

    rim = jnp.zeros((2, now.shape[1], PAD, cells_z), jnp.float32)
    now[:, :, 0:PAD, :] = rim
    now[:, :, PAD + cells_y :, :] = rim
    nxt[:, :, 0:PAD, :] = rim[:, : nxt.shape[1]]
    nxt[:, :, PAD + cells_y :, :] = rim[:, : nxt.shape[1]]
    mid_y = slice(PAD, PAD + cells_y)
    w = 2 * REACH
    now[0, w : w + extent, mid_y, :] = sn[...]
    now[1, w : w + extent, mid_y, :] = rn[...]
    pri[0, REACH : REACH + extent] = sp[...]
    pri[1, REACH : REACH + extent] = rp[...]
    vel[REACH : REACH + extent] = ve[...]

    def sides(left, right):
        for at, got in ((0, left), (1, right)):
            a = at * (w + extent)
            now[0, a : a + w, mid_y, :] = got[0:w]
            now[1, a : a + w, mid_y, :] = got[w : 2 * w]
            b = at * (REACH + extent)
            pri[0, b : b + REACH] = got[2 * w : 2 * w + REACH]
            pri[1, b : b + REACH] = got[2 * w + REACH : 3 * w]
            vel[b : b + REACH] = got[3 * w : 3 * w + REACH]

    @pl.when(odd == 0)
    def _():
        sides(far, near)

    @pl.when(odd == 1)
    def _():
        sides(near, far)

    def inject(f, t, i):
        depth = (source_depth, record_depth)[f]
        at = lax.rem(depth - (64 * t + i) + 256, 128)
        return jnp.where(lane == depth, pltpu.roll(inj[f], at, 1), 0.0)

    def first_step(i, carry):
        for f in range(2):
            mid, lap = laplace_plane(now, f, i + REACH, cells_y, lane)
            nxt[f, i, mid_y, :] = 2.0 * mid - pri[f, i] + vel[i] * lap + inject(f, 0, i)
        return carry

    lax.fori_loop(0, extent + 2 * REACH, first_step, 0)

    def second_step(i, carry):
        for f in range(2):
            mid, lap = laplace_plane(nxt, f, i + REACH, cells_y, lane)
            before = now[f, i + w, mid_y, :]
            out[f, i] = 2.0 * mid - before + vel[i + REACH] * lap + inject(f, 1, i + REACH)
        return carry

    lax.fori_loop(0, extent, second_step, 0)


def image_kernel(offsets, own, near, far, images, adj_s, adj_r, wide, squares, block, sems):
    extent = own.shape[1]
    count = images.shape[0]
    odd = lax.rem(lax.axis_index("gx"), 2)

    def fill(at, got):
        for f in range(2):
            v = got[f]
            wide[f, at : at + extent] = v
            squares[f, at : at + extent] = v * v

    fill(extent, own)

    @pl.when(odd == 0)
    def _():
        fill(0, far)
        fill(2 * extent, near)

    @pl.when(odd == 1)
    def _():
        fill(0, near)
        fill(2 * extent, far)

    def out_copy(k):
        return pltpu.make_async_copy(block.at[k], images.at[k], sems.at[k])

    def one_image(k, carry):
        shift = offsets[k]
        left = wide[0, pl.ds(extent - shift, extent)]
        right = wide[1, pl.ds(extent + shift, extent)]
        block[k] = (left * right).astype(jnp.bfloat16)
        out_copy(k).start()
        return carry

    lax.fori_loop(0, count, one_image, 0)

    def one_layer(i, carry):
        to_s = jnp.zeros(own.shape[2:], jnp.float32)
        to_r = jnp.zeros(own.shape[2:], jnp.float32)
        for k in range(count):
            shift = offsets[k]
            weight = (shift * shift).astype(jnp.float32) * (1.0 / (LAG_MAX * LAG_MAX * count))
            to_s = to_s + weight * squares[1, extent + i + 2 * shift]
            to_r = to_r + weight * squares[0, extent + i - 2 * shift]
        adj_s[i] = wide[0, extent + i] * to_s
        adj_r[i] = wide[1, extent + i] * to_r
        return carry

    lax.fori_loop(0, extent, one_layer, 0)

    def drain(k, carry):
        out_copy(k).wait()
        return carry

    lax.fori_loop(0, count, drain, 0)


def pairs(count):
    near = [(i, i ^ 1) for i in range(count)]
    far = [(i, i + 1 if i % 2 else i - 1) for i in range(count)]
    return near, [(a, b) for a, b in far if 0 <= b < count]


def per_device(
    velocity,
    source_prior,
    source_now,
    record_prior,
    record_now,
    source_inline,
    source_crossline,
    source_pulse,
    receiver_inline,
    receiver_crossline,
    receiver_trace,
    offsets,
):
    extent, cells_y, cells_z = velocity.shape
    near_pairs, far_pairs = pairs(lax.axis_size("gx"))
    fields = (velocity, source_prior, source_now, record_prior, record_now)
    f32 = functools.partial(jax.ShapeDtypeStruct, dtype=jnp.float32)
    edge = f32((7 * REACH, cells_y, cells_z))
    near, far = pl.pallas_call(
        pack_kernel,
        out_shape=(edge, edge),
        in_specs=[ANY] * 5,
        out_specs=(VMEM, VMEM),
        scratch_shapes=[pltpu.SemaphoreType.DMA((10,))],
        compiler_params=params(8),
    )(*fields)
    got_far = lax.ppermute(far, "gx", far_pairs)
    got_near = lax.ppermute(near, "gx", near_pairs)
    whole_y = cells_y + 2 * PAD
    final = pl.pallas_call(
        step_kernel,
        out_shape=f32((2, extent, cells_y, cells_z)),
        in_specs=[VMEM] * 13,
        out_specs=VMEM,
        scratch_shapes=[
            pltpu.VMEM((2, extent + 4 * REACH, whole_y, cells_z), jnp.float32),
            pltpu.VMEM((2, extent + 2 * REACH, whole_y, cells_z), jnp.float32),
            pltpu.VMEM((2, extent + 2 * REACH, cells_y, cells_z), jnp.float32),
            pltpu.VMEM((extent + 2 * REACH, cells_y, cells_z), jnp.float32),
            pltpu.VMEM((2, cells_y, cells_z), jnp.float32),
        ],
        compiler_params=params(16),
    )(
        *fields,
        got_near,
        got_far,
        source_inline[None, :],
        source_crossline[None, :],
        source_pulse.T,
        receiver_inline[None, :],
        receiver_crossline[None, :],
        receiver_trace.T,
    )
    final_far = lax.ppermute(final, "gx", far_pairs)
    final_near = lax.ppermute(final, "gx", near_pairs)
    count = offsets.shape[0]
    plane = f32((extent, cells_y, cells_z))
    return pl.pallas_call(
        image_kernel,
        out_shape=(
            jax.ShapeDtypeStruct((count, extent, cells_y, cells_z), jnp.bfloat16),
            plane,
            plane,
        ),
        in_specs=[SMEM, VMEM, VMEM, VMEM],
        out_specs=(ANY, VMEM, VMEM),
        scratch_shapes=[
            pltpu.VMEM((2, 3 * extent, cells_y, cells_z), jnp.float32),
            pltpu.VMEM((2, 3 * extent, cells_y, cells_z), jnp.float32),
            pltpu.VMEM((count, extent, cells_y, cells_z), jnp.bfloat16),
            pltpu.SemaphoreType.DMA((count,)),
        ],
        compiler_params=params(16),
    )(offsets, final, final_near, final_far)


def solution(mesh):
    in_specs = (
        P("gx", None, None),
        P(("shots", "gx"), None, None),
        P(("shots", "gx"), None, None),
        P(("shots", "gx"), None, None),
        P(("shots", "gx"), None, None),
        P("shots"),
        P("shots"),
        P("shots", None),
        P("shots"),
        P("shots"),
        P("shots", None),
        P(),
    )
    out_specs = (
        P("shots", "gx", None, None),
        P(("shots", "gx"), None, None),
        P(("shots", "gx"), None, None),
    )
    return jax.shard_map(
        per_device, mesh=mesh, in_specs=in_specs, out_specs=out_specs, check_vma=False
    )
```
